32 devices in a mesh: seg: 8 (over y, x, core), pos: 4 (over z).
Axes of the slice: x: 2, y: 2, z: 4, core: 2. Of those that a mesh axis runs over, the one named last changes fastest.
Arguments:
- query_heads: bfloat16 [32, 12, 128, 128], P('seg', None, 'pos'), may hold values from -32 to 32
- key_heads: bfloat16 [32, 12, 128, 128], P('seg', None, 'pos'), may hold values from -32 to 32
- value_heads: bfloat16 [32, 12, 128, 128], P('seg', None, 'pos'), may hold values from -6 to 6
- out_grad: bfloat16 [32, 12, 128, 128], P('seg', None, 'pos'), may hold values from -6 to 6
- clip_lengths: int32 [8], replicated, may hold values from 1 to 8, 32 in all
- clip_resolution: int32 [8], replicated, may hold values from 32 to 128
- clip_window: int32 [8], replicated, may hold values from 1 to 2
Outputs:
- grad_query: bfloat16 [32, 12, 128, 128], P('seg', None, 'pos')
- grad_key: bfloat16 [32, 12, 128, 128], P('seg', None, 'pos')
- grad_value: bfloat16 [32, 12, 128, 128], P('seg', None, 'pos')
The draws below stay inside these ranges and needn't reach their ends.
All inputs are finite; a program needn't handle non-finite values.
Results may differ from the reference program's by a relative error of at most 0.025.
Values may be sent and summed in bfloat16 or wider, within the bound.
A program may use at most 64 MiB of HBM per device.

```python
import math
import jax
import jax.numpy as jnp
import numpy as np
from jax import lax

E = 128
HEADS = 12
WMAX = 2
MAXLEN = 8
FRAMES = 32
P_SIZE = 128
CLIPS = 8


def drawn_pair(key):
    base = jax.random.fold_in(key, 11)
    key_query, key_keys = jax.random.split(base, 2)
    queries = jnp.clip(jax.random.normal(key_query, (FRAMES, HEADS, P_SIZE, E), jnp.float32), -6.0, 6.0)
    keys_drawn = jnp.clip(jax.random.normal(key_keys, (FRAMES, HEADS, P_SIZE, E), jnp.float32), -6.0, 6.0)
    return (jnp.clip(queries, -32.0, 32.0), jnp.clip(keys_drawn, -32.0, 32.0))


def draw_query_heads(key, part):
    return drawn_pair(key)[0].astype(jnp.bfloat16)


def draw_key_heads(key, part):
    return drawn_pair(key)[1].astype(jnp.bfloat16)


def draw_clip_resolution(key, part):
    base = jax.random.fold_in(key, 23)
    first, second = jax.random.split(base)
    drawn = jax.random.randint(first, (CLIPS,), P_SIZE // 4, P_SIZE + 1, jnp.int32)
    chosen = jax.random.randint(second, (), 0, CLIPS, jnp.int32)
    return jnp.where(jnp.arange(CLIPS, dtype=jnp.int32) == chosen, P_SIZE, drawn).astype(jnp.int32)


def draw_clip_window(key, part):
    base = jax.random.fold_in(key, 37)
    first, second = jax.random.split(base)
    drawn = jax.random.randint(first, (CLIPS,), 1, WMAX + 1, jnp.int32)
    chosen = jax.random.randint(second, (), 0, CLIPS, jnp.int32)
    return jnp.where(jnp.arange(CLIPS, dtype=jnp.int32) == chosen, WMAX, drawn).astype(jnp.int32)


def steps_of(rng, extent, cuts, low, largest):
    level, own = 1.0, jax.random.fold_in(rng, 6)
    for position, shards_of in cuts:
        steps = jnp.exp(jax.random.uniform(jax.random.fold_in(own, position), (shards_of,), jnp.float32, low / len(cuts), largest / len(cuts)))
        level = level * jnp.repeat(steps, extent[position] // shards_of).reshape([-1 if axis == position else 1 for axis in range(len(extent))])
    return level


def profile(amount, total, most, lean):
    portions = [(1 << 20) // math.isqrt(standing ** lean) + 1 for standing in range(2, amount + 1)]
    spare, given = total - most - (amount - 1), [1] * (amount - 1)
    while spare > 0:
        candidates = [i for i in range(amount - 1) if given[i] < most]
        whole, left = sum([portions[i] for i in candidates]), spare
        for i in candidates:
            extra = min(most - given[i], max(1, left * portions[i] // whole), spare)
            given[i] = given[i] + extra
            spare = spare - extra
    return np.array([most] + given)


def uneven(own_key, amount, total, reach, skew):
    if amount == 2:
        one = jax.random.randint(own_key, (), max(1, total - reach), min(reach, total - 1) + 1)
        return jnp.stack([one, total - one])
    lengths = jnp.asarray(profile(amount, total, reach, skew), jnp.int32)
    couples = (amount - 1) // 2
    source_of, sink = lengths[1:1 + 2 * couples:2], lengths[2:2 + 2 * couples:2]
    margin = jnp.minimum(source_of - 1, reach - sink)
    shifted = jax.random.randint(jax.random.fold_in(own_key, 1), (couples,), 0, 1 << 20) % (margin + 1)
    lengths = lengths.at[1:1 + 2 * couples:2].set(source_of - shifted).at[2:2 + 2 * couples:2].set(sink + shifted)
    return lengths[jax.random.permutation(jax.random.fold_in(own_key, 2), amount)]


def gaussian(own_key, dims, deviation, bound, cuts=(), kind=jnp.bfloat16):
    values = deviation * jax.random.normal(own_key, dims, jnp.float32)
    if cuts:
        values = values * steps_of(own_key, dims, cuts, -0.22, 0.18)
    return jnp.clip(values, -bound, bound).astype(kind)


def setup_inputs(seed: int = 0) -> dict:
    key_of = jax.random.split(jax.random.key(seed), 8)
    query_heads = draw_query_heads(jax.random.fold_in(key_of[7], 71), 0)
    key_heads = draw_key_heads(jax.random.fold_in(key_of[7], 71), 0)
    value_heads = gaussian(key_of[2], (FRAMES, HEADS, P_SIZE, E), 1.0, 6.0, ((0, 8), (2, 4)))
    out_grad = gaussian(key_of[3], (FRAMES, HEADS, P_SIZE, E), 1.0, 6.0, ((0, 8), (2, 4)))
    clip_lengths = uneven(key_of[4], CLIPS, FRAMES, MAXLEN, 2).astype(jnp.int32)
    clip_resolution = draw_clip_resolution(jax.random.fold_in(key_of[7], 71), 0)
    clip_window = draw_clip_window(jax.random.fold_in(key_of[7], 71), 0)
    return dict(query_heads=query_heads, key_heads=key_heads, value_heads=value_heads, out_grad=out_grad, clip_lengths=clip_lengths, clip_resolution=clip_resolution, clip_window=clip_window)


def frame_owner(clip_lengths, frame_total):
    clip_ends = jnp.cumsum(clip_lengths)
    frame_index = jnp.arange(frame_total, dtype=jnp.int32)
    return lax.optimization_barrier(jnp.sum((clip_ends[None, :] <= frame_index[:, None]).astype(jnp.int32), axis=1)).astype(jnp.int32)

def to_bfloat(values):
    return lax.optimization_barrier(values.astype(jnp.bfloat16)).astype(jnp.float32)

def reference(query_heads, key_heads, value_heads, out_grad, clip_lengths, clip_resolution, clip_window):
    half_heads = HEADS // 2
    inv_root = 1.0 / math.sqrt(E)
    window_len = 2 * WMAX + 1
    owner = frame_owner(clip_lengths, FRAMES)
    frame_res = clip_resolution[owner]
    frame_win = clip_window[owner]
    live_rows = jnp.arange(P_SIZE, dtype=jnp.int32)[None, :] < frame_res[:, None]
    masked_grad = jnp.where(live_rows[:, None, :, None], out_grad, jnp.zeros_like(out_grad)).astype(jnp.bfloat16)
    frame_list = jnp.arange(FRAMES, dtype=jnp.int32)

    def spatial_frame(frame_index):
        query_rows = query_heads[frame_index, :half_heads].astype(jnp.float32)
        key_rows = key_heads[frame_index, :half_heads].astype(jnp.float32)
        value_rows = value_heads[frame_index, :half_heads].astype(jnp.float32)
        cotangent = masked_grad[frame_index, :half_heads].astype(jnp.float32)
        key_live = jnp.arange(P_SIZE, dtype=jnp.int32) < frame_res[frame_index]
        scores = jnp.einsum('hie,hje->hij', query_rows, key_rows) * inv_root
        scores = jnp.where(key_live[None, None, :], scores, -jnp.inf)
        row_top = lax.optimization_barrier(jnp.max(scores, axis=2, keepdims=True))
        log_total = row_top + jnp.log(lax.optimization_barrier(jnp.sum(jnp.exp(scores - row_top), axis=2, keepdims=True)))
        weights = jnp.exp(scores - log_total)
        rounded = to_bfloat(weights)
        attended = to_bfloat(jnp.einsum('hij,hje->hie', rounded, value_rows))
        row_dot = lax.optimization_barrier(jnp.sum(cotangent * attended, axis=2, keepdims=True))
        dweights = jnp.einsum('hie,hje->hij', cotangent, value_rows)
        dscores = to_bfloat(weights * (dweights - row_dot))
        query_grad = (jnp.einsum('hij,hje->hie', dscores, key_rows) * inv_root).astype(jnp.bfloat16)
        key_grad = (jnp.einsum('hij,hie->hje', dscores, query_rows) * inv_root).astype(jnp.bfloat16)
        value_grad = jnp.einsum('hij,hie->hje', rounded, cotangent).astype(jnp.bfloat16)
        return (query_grad, key_grad, value_grad)
    spatial_q, spatial_k, spatial_v = lax.map(spatial_frame, frame_list)
    edge = jnp.full((WMAX,), -1, jnp.int32)
    owner_pad = jnp.concatenate([edge, owner, edge])
    offsets = jnp.arange(window_len, dtype=jnp.int32) - WMAX
    padding = ((WMAX, WMAX), (0, 0), (0, 0), (0, 0))
    temporal_query = query_heads[:, half_heads:]
    temporal_grad = masked_grad[:, half_heads:]
    query_pad = jnp.pad(temporal_query, padding)
    grad_pad = jnp.pad(temporal_grad, padding)
    key_pad = jnp.pad(key_heads[:, half_heads:], padding)
    value_pad = jnp.pad(value_heads[:, half_heads:], padding)

    def window_mask(frame_index):
        nearby = lax.dynamic_slice_in_dim(owner_pad, frame_index, window_len, 0)
        return (nearby == owner[frame_index]) & (jnp.abs(offsets) <= frame_win[frame_index])

    def temporal_frame(frame_index):
        query_rows = temporal_query[frame_index].astype(jnp.float32)
        key_rows = lax.dynamic_slice_in_dim(key_pad, frame_index, window_len, 0).astype(jnp.float32)
        value_rows = lax.dynamic_slice_in_dim(value_pad, frame_index, window_len, 0).astype(jnp.float32)
        cotangent = temporal_grad[frame_index].astype(jnp.float32)
        allowed = window_mask(frame_index)
        scores = jnp.einsum('hpe,dhpe->dhp', query_rows, key_rows) * inv_root
        scores = jnp.where(allowed[:, None, None], scores, -jnp.inf)
        row_top = lax.optimization_barrier(jnp.max(scores, axis=0, keepdims=True))
        log_total = row_top + jnp.log(lax.optimization_barrier(jnp.sum(jnp.exp(scores - row_top), axis=0, keepdims=True)))
        weights = jnp.exp(scores - log_total)
        rounded = to_bfloat(weights)
        attended = to_bfloat(jnp.einsum('dhp,dhpe->hpe', rounded, value_rows))
        row_dot = lax.optimization_barrier(jnp.sum(cotangent * attended, axis=2))
        dweights = jnp.einsum('hpe,dhpe->dhp', cotangent, value_rows)
        dscores = to_bfloat(weights * (dweights - row_dot[None]))
        query_grad = (jnp.einsum('dhp,dhpe->hpe', dscores, key_rows) * inv_root).astype(jnp.bfloat16)
        return (query_grad, log_total[0], row_dot)
    temporal_q, log_totals, row_dots = lax.map(temporal_frame, frame_list)
    stat_padding = ((WMAX, WMAX), (0, 0), (0, 0))
    total_pad = jnp.pad(log_totals, stat_padding)
    dot_pad = jnp.pad(row_dots, stat_padding)

    def key_frame(frame_index):
        key_rows = key_heads[frame_index, half_heads:].astype(jnp.float32)
        value_rows = value_heads[frame_index, half_heads:].astype(jnp.float32)
        query_rows = lax.dynamic_slice_in_dim(query_pad, frame_index, window_len, 0).astype(jnp.float32)
        cotangent = lax.dynamic_slice_in_dim(grad_pad, frame_index, window_len, 0).astype(jnp.float32)
        totals = lax.dynamic_slice_in_dim(total_pad, frame_index, window_len, 0)
        products = lax.dynamic_slice_in_dim(dot_pad, frame_index, window_len, 0)
        allowed = window_mask(frame_index)
        scores = jnp.einsum('dhpe,hpe->dhp', query_rows, key_rows) * inv_root
        weights = jnp.where(allowed[:, None, None], jnp.exp(scores - totals), jnp.zeros_like(scores))
        rounded = to_bfloat(weights)
        dweights = jnp.einsum('dhpe,hpe->dhp', cotangent, value_rows)
        dscores = to_bfloat(weights * (dweights - products))
        key_grad = (jnp.einsum('dhp,dhpe->hpe', dscores, query_rows) * inv_root).astype(jnp.bfloat16)
        value_grad = jnp.einsum('dhp,dhpe->hpe', rounded, cotangent).astype(jnp.bfloat16)
        return (key_grad, value_grad)
    temporal_k, temporal_v = lax.map(key_frame, frame_list)
    grad_query = jnp.concatenate([spatial_q, temporal_q], axis=1)
    grad_key = jnp.concatenate([spatial_k, temporal_k], axis=1)
    grad_value = jnp.concatenate([spatial_v, temporal_v], axis=1)
    return (grad_query, grad_key, grad_value)
```

```python
import functools
import math

import jax
import jax.numpy as jnp
from jax import lax
from jax.experimental import pallas as pl
from jax.experimental.pallas import tpu as pltpu
from jax.sharding import PartitionSpec as P

WMAX = 2
MESH = pl.DeviceIdType.MESH
CHUNK = 3
AHEAD = 2
FAR = -1e30


def matmul(left, right, dims):
    return lax.dot_general(left, right, (dims, ((), ())), preferred_element_type=jnp.float32)


def kernel(
    n,
    segs,
    chunk,
    q_ref,
    k_ref,
    v_ref,
    g_ref,
    len_ref,
    res_ref,
    win_ref,
    oq_ref,
    ok_ref,
    ov_ref,
    qg,
    kv,
    powers_of,
    slopes,
    mine,
    theirs,
    part,
    cast,
    given,
    back,
    tqg,
    ekv,
    edge,
    redge,
    own,
    up_s,
    up_r,
    over_s,
    over_r,
    stat_s,
    stat_r,
    part_s,
    part_r,
    down_s,
    down_r,
    halo_s,
    halo_r,
    ret_s,
    ret_r,
    in_s,
    out_s,
    time_s,
):
    frames, heads, rows, width = q_ref.shape
    half = heads // 2
    pieces = frames * half // chunk
    groups = half // chunk
    m = n // 2
    keys_held = m * rows
    positions = n * rows
    inv_root = 1.0 / math.sqrt(width)
    ins = (q_ref, g_ref, k_ref, v_ref)
    outs = (oq_ref, ok_ref, ov_ref)
    seg = lax.axis_index("seg")
    pos = lax.axis_index("pos")
    right = lax.rem(seg + 1, segs)
    left = lax.rem(seg + segs - 1, segs)
    side = lax.div(pos, m)
    spot = pos - side * m
    hub_spot = (m - 1) * (1 - side)
    hub = side * m + hub_spot
    peer = n - 1 - hub
    peer_spot = (m - 1) * side
    is_hub = pos == hub

    def rows_of(p):
        return pl.ds(pl.multiple_of(p * rows, rows), rows)

    def half_of(p):
        return pl.ds(pl.multiple_of(p * keys_held, keys_held), keys_held)

    def block(ref, piece):
        return ref.at[piece // groups, pl.ds(piece % groups * chunk, chunk)]

    def span(piece):
        return pl.ds(piece * chunk, chunk)

    def slot(a, piece, spot):
        if a < 2:
            return qg.at[a, span(piece), rows_of(side * m + spot)]
        return kv.at[a - 2, span(piece), rows_of(spot)]

    def remote(src, dst, send, recv, dest):
        return pltpu.make_async_remote_copy(
            src_ref=src,
            dst_ref=dst,
            send_sem=send,
            recv_sem=recv,
            device_id=(seg, dest),
            device_id_type=MESH,
        )

    def up(a, piece, spot):
        return remote(
            block(ins[a], piece),
            slot(a, piece, spot),
            up_s.at[a, piece],
            up_r.at[a, piece, spot],
            hub,
        )

    def over(a, piece, spot, where, source):
        return remote(
            source,
            qg.at[a, span(piece), rows_of(where * m + spot)],
            over_s.at[a, piece, spot],
            over_r.at[a, piece, spot],
            peer,
        )

    def over_own(a, piece):
        return over(a, piece, hub_spot, side, block(ins[a], piece))

    def over_next(a, piece, spot):
        return over(a, piece, spot, side, slot(a, piece, spot))

    def over_in(a, piece, spot):
        return over(a, piece, spot, 1 - side, block(ins[a], piece))

    def stat(piece):
        return remote(mine.at[piece], theirs.at[piece], stat_s.at[piece], stat_r.at[piece], peer)

    def cross(piece):
        return remote(
            cast.at[span(piece), half_of(1 - side)],
            given.at[span(piece)],
            part_s.at[piece],
            part_r.at[piece],
            peer,
        )

    def down(a, piece, spot, dest):
        return remote(
            back.at[a, span(piece), rows_of(spot)],
            block(outs[a], piece),
            down_s.at[a, piece, spot],
            down_r.at[a, piece],
            dest,
        )

    def self_in(a, piece):
        return pltpu.make_async_copy(
            block(ins[a], piece), slot(a, piece, hub_spot), in_s.at[a, piece]
        )

    def self_out(a, piece):
        return pltpu.make_async_copy(
            back.at[a, span(piece), rows_of(hub_spot)], block(outs[a], piece), out_s.at[a, piece]
        )

    def time_half(ref, first, count):
        return ref.at[pl.ds(first, count), pl.ds(half, half)]

    def halo(way, a):
        source = (k_ref, v_ref)[a]
        if way == 0:
            src, dst, dest = time_half(source, frames - WMAX, WMAX), 0, right
        else:
            src, dst, dest = time_half(source, 0, WMAX), frames + WMAX, left
        return pltpu.make_async_remote_copy(
            src_ref=src,
            dst_ref=ekv.at[a, pl.ds(dst, WMAX)],
            send_sem=halo_s.at[way, a],
            recv_sem=halo_r.at[way, a],
            device_id=(dest, pos),
            device_id_type=MESH,
        )

    def give(way):
        return pltpu.make_async_remote_copy(
            src_ref=edge.at[way],
            dst_ref=redge.at[way],
            send_sem=ret_s.at[way],
            recv_sem=ret_r.at[way],
            device_id=((left, right)[way], pos),
            device_id_type=MESH,
        )

    time_in = [
        pltpu.make_async_copy(time_half(q_ref, 0, frames), tqg.at[0], time_s.at[0]),
        pltpu.make_async_copy(time_half(g_ref, 0, frames), tqg.at[1], time_s.at[1]),
        pltpu.make_async_copy(
            time_half(k_ref, 0, frames), ekv.at[0, pl.ds(WMAX, frames)], time_s.at[2]
        ),
        pltpu.make_async_copy(
            time_half(v_ref, 0, frames), ekv.at[1, pl.ds(WMAX, frames)], time_s.at[3]
        ),
    ]

    others = [lax.rem(hub_spot + r, m) for r in range(1, m)]
    peers_others = [lax.rem(peer_spot + r, m) for r in range(1, m)]
    barrier = pltpu.get_barrier_semaphore()

    def greet(where, dest):
        pl.semaphore_signal(barrier, inc=1, device_id=(where, dest), device_id_type=MESH)

    for near in (left, right):
        greet(near, pos)

    @pl.when(is_hub)
    def _():
        greet(seg, peer)
        for spot in others:
            greet(seg, side * m + spot)
        for piece in range(pieces):
            for a in range(4):
                self_in(a, piece).start()

    @pl.when(jnp.logical_not(is_hub))
    def _():
        greet(seg, hub)

    for copy in time_in:
        copy.start()

    @pl.when(is_hub)
    def _():
        pl.semaphore_wait(barrier, m + 2)
        for piece in range(min(2 * AHEAD, pieces)):
            for a in range(2):
                over_own(a, piece).start()

    @pl.when(jnp.logical_not(is_hub))
    def _():
        pl.semaphore_wait(barrier, 3)
        for piece in range(pieces):
            for a in range(4):
                up(a, piece, spot).start()

    for way in range(2):
        for a in range(2):
            halo(way, a).start()

    ext = frames + 2 * WMAX
    base = seg * frames
    zero = jnp.int32(0)

    def clip_step(c, carry):
        start, owners, live, wins = carry
        end = start + len_ref[c]
        owners = tuple(
            o + jnp.where(end <= base + (x - WMAX), 1, 0) for x, o in enumerate(owners)
        )
        inside = [(start <= base + x) & (base + x < end) for x in range(frames)]
        live = tuple(jnp.where(i, res_ref[c], o) for i, o in zip(inside, live))
        wins = tuple(jnp.where(i, win_ref[c], o) for i, o in zip(inside, wins))
        return end, owners, live, wins

    _, owners, live, wins = lax.fori_loop(
        0, len_ref.shape[0], clip_step, (zero, (zero,) * ext, (zero,) * frames, (zero,) * frames)
    )
    owners = [jnp.where(base + (x - WMAX) < 0, -1, o) for x, o in enumerate(owners)]
    bias = [
        [
            jnp.where(
                (owners[i + o] == owners[i + WMAX]) & (wins[i] >= abs(o - WMAX)), 0.0, -jnp.inf
            ).astype(jnp.float32)
            for o in range(2 * WMAX + 1)
        ]
        for i in range(frames)
    ]

    def time_head(h, carry):
        row = lax.broadcasted_iota(jnp.int32, (rows, 1), 0) + pos * rows
        keys = [ekv[0, j, h].astype(jnp.float32) for j in range(ext)]
        values = [ekv[1, j, h].astype(jnp.float32) for j in range(ext)]
        key_sum = [None] * ext
        value_sum = [None] * ext
        for i in range(frames):
            query = tqg[0, i, h].astype(jnp.float32)
            grad = tqg[1, i, h].astype(jnp.float32)
            offsets = range(2 * WMAX + 1)
            scores = [
                jnp.sum(query * keys[i + o], axis=1, keepdims=True) * inv_root + bias[i][o]
                for o in offsets
            ]
            dweights = [jnp.sum(grad * values[i + o], axis=1, keepdims=True) for o in offsets]
            top = functools.reduce(jnp.maximum, scores)
            powers = [jnp.exp(s - top) for s in scores]
            scale = jnp.where(row < live[i], 1.0 / sum(powers[1:], powers[0]), 0.0)
            weights = [p * scale for p in powers]
            low = [w.astype(jnp.bfloat16).astype(jnp.float32) for w in weights]
            dots = [w * d for w, d in zip(low, dweights)]
            row_dot = sum(dots[1:], dots[0])
            dscores = [
                (w * (d - row_dot)).astype(jnp.bfloat16).astype(jnp.float32)
                for w, d in zip(weights, dweights)
            ]
            terms = [dscores[o] * keys[i + o] for o in offsets]
            oq_ref[i, half + h] = (sum(terms[1:], terms[0]) * inv_root).astype(jnp.bfloat16)
            for o in offsets:
                j = i + o
                key_term = dscores[o] * query
                value_term = low[o] * grad
                key_sum[j] = key_term if key_sum[j] is None else key_sum[j] + key_term
                value_sum[j] = value_term if value_sum[j] is None else value_sum[j] + value_term
        for a, sums in enumerate((key_sum, value_sum)):
            factor = inv_root if a == 0 else 1.0
            for j in range(WMAX):
                edge[0, a, j, h] = (sums[j] * factor).astype(jnp.bfloat16)
                edge[1, a, j, h] = (sums[frames + WMAX + j] * factor).astype(jnp.bfloat16)
            for i in range(frames):
                own[a, i, h] = sums[WMAX + i] * factor
        return carry

    def time_close(h, carry):
        for a in range(2):
            for i in range(frames):
                total = own[a, i, h]
                if i < WMAX:
                    total = total + redge[1, a, i, h].astype(jnp.float32)
                if i >= frames - WMAX:
                    total = total + redge[0, a, i - (frames - WMAX), h].astype(jnp.float32)
                outs[1 + a][i, half + h] = total.astype(jnp.bfloat16)
        return carry

    def time_begin():
        for copy in time_in:
            copy.wait()
        for way in range(2):
            for a in range(2):
                halo(way, a).wait_recv()

    def time_send():
        for way in range(2):
            give(way).start()

    def time_end():
        for way in range(2):
            give(way).wait_recv()
        lax.fori_loop(0, half, time_close, 0)

    def pass_on(piece):
        for a in range(2):
            for spot in others:
                up(a, piece, spot).wait_recv()
                over_next(a, piece, spot).start()

    def score(piece):
        for a in range(4):
            self_in(a, piece).wait()
            if a >= 2:
                for spot in others:
                    up(a, piece, spot).wait_recv()
        for a in range(2):
            over_in(a, piece, peer_spot).wait_recv()
            for spot in peers_others:
                over_in(a, piece, spot).wait_recv()
        limit = live[piece // groups]
        key = lax.broadcasted_iota(jnp.int32, (keys_held, 1), 0) + side * keys_held
        for i in range(chunk):
            t = piece * chunk + i
            scores = matmul(kv[0, t], qg[0, t], ((1,), (1,))) * inv_root
            scores = jnp.where(key < limit, scores, FAR)
            top = jnp.max(scores, axis=0, keepdims=True)
            powers = jnp.exp(scores - top)
            dweights = matmul(kv[1, t], qg[1, t], ((1,), (1,)))
            powers_of[t] = powers
            slopes[t] = dweights
            mine[piece, pl.ds(i, 1)] = top
            mine[piece, pl.ds(chunk + i, 1)] = jnp.sum(powers, axis=0, keepdims=True)
            mine[piece, pl.ds(2 * chunk + i, 1)] = jnp.sum(powers * dweights, axis=0, keepdims=True)
        stat(piece).start()

    def solve(piece):
        stat(piece).wait_recv()
        limit = live[piece // groups]
        query = lax.broadcasted_iota(jnp.int32, (1, positions), 1)
        for i in range(chunk):
            t = piece * chunk + i
            top, total, dot = (mine[piece, pl.ds(k * chunk + i, 1)] for k in range(3))
            top_in, total_in, dot_in = (theirs[piece, pl.ds(k * chunk + i, 1)] for k in range(3))
            high = jnp.maximum(top, top_in)
            low_in = jnp.exp(top_in - high)
            low_own = jnp.exp(top - high)
            inverse = 1.0 / (total * low_own + total_in * low_in)
            row_dot = (dot * low_own + dot_in * low_in) * inverse
            weights = powers_of[t] * jnp.where(query < limit, low_own * inverse, 0.0)
            dscores = (weights * (slopes[t] - row_dot)).astype(jnp.bfloat16)
            query_part = matmul(dscores, kv[0, t], ((0,), (0,))) * inv_root
            part[t] = query_part
            cast[t] = query_part.astype(jnp.bfloat16)
            key_part = matmul(dscores, qg[0, t], ((1,), (0,))) * inv_root
            back[1, t] = key_part.astype(jnp.bfloat16)
            value_part = matmul(weights.astype(jnp.bfloat16), qg[1, t], ((1,), (0,)))
            back[2, t] = value_part.astype(jnp.bfloat16)
        cross(piece).start()
        for a in (1, 2):
            hand(a, piece)

    def hand(a, piece):
        for spot in others:
            down(a, piece, spot, side * m + spot).start()
        self_out(a, piece).start()

    def settle(piece):
        cross(piece).wait_recv()
        for i in range(chunk):
            t = piece * chunk + i
            total = part[t, half_of(side)] + given[t].astype(jnp.float32)
            back[0, t] = total.astype(jnp.bfloat16)
        hand(0, piece)

    @pl.when(is_hub)
    def _():
        for piece in range(min(AHEAD, pieces)):
            pass_on(piece)
        for piece in range(2 * AHEAD, min(3 * AHEAD, pieces)):
            for a in range(2):
                over_own(a, piece).start()
        busy = max(1, pieces - 2)
        for piece in range(pieces):
            score(piece)
            if piece + AHEAD < pieces:
                pass_on(piece + AHEAD)
            if piece + 3 * AHEAD < pieces:
                for a in range(2):
                    over_own(a, piece + 3 * AHEAD).start()
            if piece == 0:
                time_begin()
            if piece < busy:
                lax.fori_loop(piece * half // busy, (piece + 1) * half // busy, time_head, 0)
            if piece == busy - 1:
                time_send()
            if piece == pieces - 1:
                time_end()
            solve(piece)
            if piece > 0:
                settle(piece - 1)
        settle(pieces - 1)

        for piece in range(pieces):
            stat(piece).wait_send()
            cross(piece).wait_send()
            for a in range(2):
                over_own(a, piece).wait_send()
                for spot in others:
                    over_next(a, piece, spot).wait_send()
            for a in range(3):
                self_out(a, piece).wait()
                for spot in others:
                    down(a, piece, spot, side * m + spot).wait_send()

    @pl.when(jnp.logical_not(is_hub))
    def _():
        time_begin()
        lax.fori_loop(0, half, time_head, 0)
        time_send()
        time_end()
        for piece in range(pieces):
            for a in range(4):
                up(a, piece, spot).wait_send()
            for a in range(3):
                down(a, piece, spot, hub).wait_recv()

    for way in range(2):
        give(way).wait_send()
        for a in range(2):
            halo(way, a).wait_send()


def put_out(*refs):
    count = (len(refs) - 1) // 2
    copies = [
        pltpu.make_async_copy(refs[a], refs[count + a], refs[-1].at[a]) for a in range(count)
    ]
    for copy in copies:
        copy.start()
    for copy in copies:
        copy.wait()


def solution(mesh):
    n, segs = mesh.shape["pos"], mesh.shape["seg"]

    def on_device(*args):
        frames, heads, rows, width = args[0].shape
        half = heads // 2
        items = frames * half
        chunk = max(c for c in range(1, CHUNK + 1) if half % c == 0)
        pieces = items // chunk
        m = n // 2
        low = jnp.bfloat16
        block = (half, rows, width)
        any_spec = pl.BlockSpec(memory_space=pl.ANY)
        smem_spec = pl.BlockSpec(memory_space=pltpu.SMEM)
        dma = pltpu.SemaphoreType.DMA
        out = jax.ShapeDtypeStruct(args[0].shape, low)
        vmem_out = pltpu.VMEM(args[0].shape, low)
        vmem_spec = pl.BlockSpec(memory_space=pltpu.VMEM)
        grads = pl.pallas_call(
            functools.partial(kernel, n, segs, chunk),
            out_shape=(vmem_out,) * 3,
            in_specs=[any_spec] * 4 + [smem_spec] * 3,
            out_specs=(vmem_spec,) * 3,
            scratch_shapes=[
                pltpu.VMEM((2, items, n * rows, width), low),
                pltpu.VMEM((2, items, m * rows, width), low),
                pltpu.VMEM((items, m * rows, n * rows), jnp.float32),
                pltpu.VMEM((items, m * rows, n * rows), jnp.float32),
                pltpu.VMEM((pieces, 3 * chunk, n * rows), jnp.float32),
                pltpu.VMEM((pieces, 3 * chunk, n * rows), jnp.float32),
                pltpu.VMEM((items, n * rows, width), jnp.float32),
                pltpu.VMEM((items, n * rows, width), low),
                pltpu.VMEM((items, m * rows, width), low),
                pltpu.VMEM((3, items, m * rows, width), low),
                pltpu.VMEM((2, frames) + block, low),
                pltpu.VMEM((2, frames + 2 * WMAX) + block, low),
                pltpu.VMEM((2, 2, WMAX) + block, low),
                pltpu.VMEM((2, 2, WMAX) + block, low),
                pltpu.VMEM((2, frames) + block, jnp.float32),
                dma((4, pieces)),
                dma((4, pieces, m)),
                dma((2, pieces, m)),
                dma((2, pieces, m)),
                dma((pieces,)),
                dma((pieces,)),
                dma((pieces,)),
                dma((pieces,)),
                dma((3, pieces, m)),
                dma((3, pieces)),
                dma((2, 2)),
                dma((2, 2)),
                dma((2,)),
                dma((2,)),
                dma((4, pieces)),
                dma((3, pieces)),
                dma((4,)),
            ],
            compiler_params=pltpu.CompilerParams(collective_id=0, has_side_effects=True),
        )(*args)
        return pl.pallas_call(
            put_out,
            out_shape=(out, out, out),
            in_specs=[vmem_spec] * 3,
            out_specs=(any_spec,) * 3,
            scratch_shapes=[dma((3,))],
        )(*(pltpu.with_memory_space_constraint(x, pltpu.VMEM) for x in grads))

    heads_spec = P("seg", None, "pos", None)
    return jax.shard_map(
        on_device,
        mesh=mesh,
        in_specs=(heads_spec,) * 4 + (P(),) * 3,
        out_specs=(heads_spec,) * 3,
        check_vma=False,
    )
```

```python
import functools
import math

import jax
import jax.numpy as jnp
from jax import lax
from jax.experimental import pallas as pl
from jax.experimental.pallas import tpu as pltpu
from jax.sharding import PartitionSpec as P

WMAX = 2
MESH = pl.DeviceIdType.MESH
PARTS = 1


def matmul(left, right, dims):
    return lax.dot_general(left, right, (dims, ((), ())), preferred_element_type=jnp.float32)


def kernel(
    n,
    segs,
    chunk,
    q_ref,
    k_ref,
    v_ref,
    g_ref,
    len_ref,
    res_ref,
    win_ref,
    oq_ref,
    ok_ref,
    ov_ref,
    recv,
    back,
    saved,
    slopes,
    tqg,
    ekv,
    edge,
    redge,
    own,
    fwd_s,
    fwd_r,
    back_s,
    back_r,
    halo_s,
    halo_r,
    ret_s,
    ret_r,
    self_s,
    time_s,
    known_s,
    beside_s,
):
    frames, heads, rows, width = q_ref.shape
    half = heads // 2
    items = frames * half // n
    pieces = items // chunk
    positions = n * rows
    inv_root = 1.0 / math.sqrt(width)
    ins = (q_ref, k_ref, v_ref, g_ref)
    outs = (oq_ref, ok_ref, ov_ref)
    seg = lax.axis_index("seg")
    pos = lax.axis_index("pos")
    right = lax.rem(seg + 1, segs)
    left = lax.rem(seg + segs - 1, segs)
    middle = n // 2
    upper = pos >= middle
    steps = range(1, n)
    targets = [
        jnp.where(
            upper,
            jnp.where(i < pos, i, i + 1),
            jnp.where(n - 1 - i > pos, n - 1 - i, n - 2 - i),
        )
        for i in range(n - 1)
    ]

    def rows_of(p):
        return pl.ds(pl.multiple_of(p * rows, rows), rows)

    def item_block(ref, owner, piece):
        first = owner * items + piece * chunk
        return ref.at[lax.div(first, half), pl.ds(lax.rem(first, half), chunk)]

    def fwd(a, piece, dest, source):
        return pltpu.make_async_remote_copy(
            src_ref=item_block(ins[a], dest, piece),
            dst_ref=recv.at[a, pl.ds(piece * chunk, chunk), rows_of(source)],
            send_sem=fwd_s.at[a, piece, dest],
            recv_sem=fwd_r.at[a, piece, source],
            device_id=(seg, dest),
            device_id_type=MESH,
        )

    def backward(a, piece, dest, source):
        return pltpu.make_async_remote_copy(
            src_ref=back.at[a, pl.ds(piece * chunk, chunk), rows_of(dest)],
            dst_ref=item_block(outs[a], source, piece),
            send_sem=back_s.at[a, piece, dest],
            recv_sem=back_r.at[a, piece, source],
            device_id=(seg, dest),
            device_id_type=MESH,
        )

    def self_in(a, piece):
        return pltpu.make_async_copy(
            item_block(ins[a], pos, piece),
            recv.at[a, pl.ds(piece * chunk, chunk), rows_of(pos)],
            self_s.at[a, piece],
        )

    def self_out(a, piece):
        return pltpu.make_async_copy(
            back.at[a, pl.ds(piece * chunk, chunk), rows_of(pos)],
            item_block(outs[a], pos, piece),
            self_s.at[4 + a, piece],
        )

    def time_half(ref, first, count):
        return ref.at[pl.ds(first, count), pl.ds(half, half)]

    def halo(way, a):
        source = (k_ref, v_ref)[a]
        if way == 0:
            src, dst, dest = time_half(source, frames - WMAX, WMAX), 0, right
        else:
            src, dst, dest = time_half(source, 0, WMAX), frames + WMAX, left
        return pltpu.make_async_remote_copy(
            src_ref=src,
            dst_ref=ekv.at[a, pl.ds(dst, WMAX)],
            send_sem=halo_s.at[way, a],
            recv_sem=halo_r.at[way, a],
            device_id=(dest, pos),
            device_id_type=MESH,
        )

    def give(way):
        return pltpu.make_async_remote_copy(
            src_ref=edge.at[way],
            dst_ref=redge.at[way],
            send_sem=ret_s.at[way],
            recv_sem=ret_r.at[way],
            device_id=((left, right)[way], pos),
            device_id_type=MESH,
        )

    time_in = [
        pltpu.make_async_copy(time_half(q_ref, 0, frames), tqg.at[0], time_s.at[0]),
        pltpu.make_async_copy(time_half(g_ref, 0, frames), tqg.at[1], time_s.at[1]),
        pltpu.make_async_copy(
            time_half(k_ref, 0, frames), ekv.at[0, pl.ds(WMAX, frames)], time_s.at[2]
        ),
        pltpu.make_async_copy(
            time_half(v_ref, 0, frames), ekv.at[1, pl.ds(WMAX, frames)], time_s.at[3]
        ),
    ]

    barrier = pltpu.get_barrier_semaphore()
    even = lax.rem(seg, 2) == 0
    inward = jnp.where(upper, pos - 1, pos + 1)
    outward = jnp.where(upper, pos + 1, pos - 1)
    centre = (pos == middle - 1) | (pos == middle)
    rim = (pos == 0) | (pos == n - 1)

    def signal(sem, where, dest):
        pl.semaphore_signal(sem, inc=1, device_id=(where, dest), device_id_type=MESH)

    @pl.when(centre)
    def _():
        signal(barrier, seg, inward)

    @pl.when(jnp.logical_not(rim))
    def _():
        signal(barrier, seg, outward)

    @pl.when(even)
    def _():
        for beside in (left, right):
            signal(barrier, beside, pos)

    for copy in time_in:
        copy.start()
    for piece in range(pieces):
        for a in range(4):
            self_in(a, piece).start()

    @pl.when(even)
    def _():
        pl.semaphore_wait(barrier, 1)

    @pl.when(jnp.logical_not(even))
    def _():
        pl.semaphore_wait(barrier, 3)

    def push(arrays, dest):
        for piece in range(pieces):
            for a in arrays:
                fwd(a, piece, dest, pos).start()

    push((0, 1, 3), inward)

    @pl.when(jnp.logical_not(centre))
    def _():
        signal(known_s.at[jnp.where(upper, 1, 0), 1], seg, inward)

    @pl.when(jnp.logical_not(even))
    def _():
        signal(beside_s.at[1], left, pos)
        signal(beside_s.at[0], right, pos)

    @pl.when(jnp.logical_not(rim))
    def _():
        pl.semaphore_wait(known_s.at[jnp.where(upper, 1, 0), 1], 1)
        push((0, 1), outward)

    def present(way, reach):
        return pos >= reach if way == 0 else pos + reach < n

    def relay(way, reach):
        if reach + 1 < n:

            @pl.when(present(1 - way, 1))
            def _():
                signal(known_s.at[way, reach + 1], seg, pos + 1 - 2 * way)

    for way in range(2):

        @pl.when(present(way, 1))
        def _():
            relay(way, 1)

    @pl.when(even)
    def _():
        for way in range(2):
            pl.semaphore_wait(beside_s.at[way], 1)

    for way in range(2):
        for a in range(2):
            halo(way, a).start()

    for reach in range(2, n):
        for way in range(2):

            @pl.when(present(way, reach))
            def _():
                pl.semaphore_wait(known_s.at[way, reach], 1)
                relay(way, reach)
                push((0, 1), pos + (2 * way - 1) * reach)

    for a in (3, 2):
        for dest in targets:
            if a == 2:
                push((a,), dest)
            else:

                @pl.when(dest != inward)
                def _():
                    push((a,), dest)

    ext = frames + 2 * WMAX
    base = seg * frames
    zero = jnp.int32(0)

    def clip_step(c, carry):
        start, owners, live, wins = carry
        end = start + len_ref[c]
        owners = tuple(
            o + jnp.where(end <= base + (x - WMAX), 1, 0) for x, o in enumerate(owners)
        )
        inside = [(start <= base + x) & (base + x < end) for x in range(frames)]
        live = tuple(jnp.where(i, res_ref[c], o) for i, o in zip(inside, live))
        wins = tuple(jnp.where(i, win_ref[c], o) for i, o in zip(inside, wins))
        return end, owners, live, wins

    _, owners, live, wins = lax.fori_loop(
        0, len_ref.shape[0], clip_step, (zero, (zero,) * ext, (zero,) * frames, (zero,) * frames)
    )
    owners = [jnp.where(base + (x - WMAX) < 0, -1, o) for x, o in enumerate(owners)]
    bias = [
        [
            jnp.where(
                (owners[i + o] == owners[i + WMAX]) & (wins[i] >= abs(o - WMAX)), 0.0, -jnp.inf
            ).astype(jnp.float32)
            for o in range(2 * WMAX + 1)
        ]
        for i in range(frames)
    ]

    for copy in time_in:
        copy.wait()
    for way in range(2):
        for a in range(2):
            halo(way, a).wait_recv()

    def time_head(h, carry):
        row = lax.broadcasted_iota(jnp.int32, (rows, 1), 0) + pos * rows
        keys = [ekv[0, j, h].astype(jnp.float32) for j in range(ext)]
        values = [ekv[1, j, h].astype(jnp.float32) for j in range(ext)]
        key_sum = [None] * ext
        value_sum = [None] * ext
        for i in range(frames):
            query = tqg[0, i, h].astype(jnp.float32)
            grad = tqg[1, i, h].astype(jnp.float32)
            offsets = range(2 * WMAX + 1)
            scores = [
                jnp.sum(query * keys[i + o], axis=1, keepdims=True) * inv_root + bias[i][o]
                for o in offsets
            ]
            dweights = [jnp.sum(grad * values[i + o], axis=1, keepdims=True) for o in offsets]
            top = functools.reduce(jnp.maximum, scores)
            powers = [jnp.exp(s - top) for s in scores]
            scale = jnp.where(row < live[i], 1.0 / sum(powers[1:], powers[0]), 0.0)
            weights = [p * scale for p in powers]
            low = [w.astype(jnp.bfloat16).astype(jnp.float32) for w in weights]
            dots = [w * d for w, d in zip(low, dweights)]
            row_dot = sum(dots[1:], dots[0])
            dscores = [
                (w * (d - row_dot)).astype(jnp.bfloat16).astype(jnp.float32)
                for w, d in zip(weights, dweights)
            ]
            terms = [dscores[o] * keys[i + o] for o in offsets]
            oq_ref[i, half + h] = (sum(terms[1:], terms[0]) * inv_root).astype(jnp.bfloat16)
            for o in offsets:
                j = i + o
                key_term = dscores[o] * query
                value_term = low[o] * grad
                key_sum[j] = key_term if key_sum[j] is None else key_sum[j] + key_term
                value_sum[j] = value_term if value_sum[j] is None else value_sum[j] + value_term
        for a, sums in enumerate((key_sum, value_sum)):
            factor = inv_root if a == 0 else 1.0
            for j in range(WMAX):
                edge[0, a, j, h] = (sums[j] * factor).astype(jnp.bfloat16)
                edge[1, a, j, h] = (sums[frames + WMAX + j] * factor).astype(jnp.bfloat16)
            for i in range(frames):
                own[a, i, h] = sums[WMAX + i] * factor
        return carry

    lax.fori_loop(0, half, time_head, 0)
    for way in range(2):
        give(way).start()

    def arrived(a, piece):
        self_in(a, piece).wait()
        for r in steps:
            source = lax.rem(pos + r, n)
            fwd(a, piece, source, source).wait_recv()

    def send(a, piece):
        for dest in targets:
            backward(a, piece, dest, pos).start()
        self_out(a, piece).start()

    for piece in range(pieces):
        span = range(piece * chunk, (piece + 1) * chunk)
        arrived(0, piece)
        arrived(1, piece)
        for t in span:
            frame = lax.div(pos * items + t, half)
            limit = sum(
                (jnp.where(frame == i, live[i], 0) for i in range(1, frames)),
                jnp.where(frame == 0, live[0], 0),
            )
            row = lax.broadcasted_iota(jnp.int32, (positions, 1), 0)
            col = lax.broadcasted_iota(jnp.int32, (1, positions), 1)
            scores = matmul(recv[0, t], recv[1, t], ((1,), (1,))) * inv_root
            scores = jnp.where(col < limit, scores, -jnp.inf)
            powers = jnp.exp(scores - jnp.max(scores, axis=1, keepdims=True))
            total = jnp.sum(powers, axis=1, keepdims=True)
            saved[t] = powers * jnp.where(row < limit, 1.0 / total, 0.0)
        arrived(3, piece)
        for t in span:
            low = saved[t].astype(jnp.bfloat16)
            back[2, t] = matmul(low, recv[3, t], ((0,), (0,))).astype(jnp.bfloat16)
        send(2, piece)
        arrived(2, piece)
        for t in span:
            weights = saved[t]
            low = weights.astype(jnp.bfloat16).astype(jnp.float32)
            dweights = matmul(recv[3, t], recv[2, t], ((1,), (1,)))
            row_dot = jnp.sum(low * dweights, axis=1, keepdims=True)
            dscores = (weights * (dweights - row_dot)).astype(jnp.bfloat16)
            slopes[t] = dscores
            query_part = matmul(dscores, recv[1, t], ((1,), (0,))) * inv_root
            back[0, t] = query_part.astype(jnp.bfloat16)
        send(0, piece)
        for t in span:
            key_part = matmul(slopes[t], recv[0, t], ((0,), (0,))) * inv_root
            back[1, t] = key_part.astype(jnp.bfloat16)
        send(1, piece)

    for way in range(2):
        give(way).wait_recv()

    def time_close(h, carry):
        for a in range(2):
            for i in range(frames):
                total = own[a, i, h]
                if i < WMAX:
                    total = total + redge[1, a, i, h].astype(jnp.float32)
                if i >= frames - WMAX:
                    total = total + redge[0, a, i - (frames - WMAX), h].astype(jnp.float32)
                outs[1 + a][i, half + h] = total.astype(jnp.bfloat16)
        return carry

    lax.fori_loop(0, half, time_close, 0)

    for way in range(2):
        give(way).wait_send()
        for a in range(2):
            halo(way, a).wait_send()
    for piece in range(pieces):
        for r in steps:
            other = lax.rem(pos + r, n)
            for a in range(4):
                fwd(a, piece, other, pos).wait_send()
            for a in range(3):
                backward(a, piece, other, pos).wait_send()
    for piece in range(pieces):
        for a in range(3):
            self_out(a, piece).wait()
            for r in steps:
                source = lax.rem(pos + r, n)
                backward(a, piece, source, source).wait_recv()


def put_out(*refs):
    count = (len(refs) - 1) // 2
    copies = [
        pltpu.make_async_copy(refs[a], refs[count + a], refs[-1].at[a]) for a in range(count)
    ]
    for copy in copies:
        copy.start()
    for copy in copies:
        copy.wait()


def solution(mesh):
    n, segs = mesh.shape["pos"], mesh.shape["seg"]

    def on_device(*args):
        frames, heads, rows, width = args[0].shape
        half = heads // 2
        items = frames * half // n
        limit = max(1, items // PARTS)
        chunk = max(c for c in range(1, limit + 1) if items % c == 0 and half % c == 0)
        pieces = items // chunk
        low = jnp.bfloat16
        block = (half, rows, width)
        any_spec = pl.BlockSpec(memory_space=pl.ANY)
        smem_spec = pl.BlockSpec(memory_space=pltpu.SMEM)
        dma = pltpu.SemaphoreType.DMA
        out = jax.ShapeDtypeStruct(args[0].shape, low)
        vmem_out = pltpu.VMEM(args[0].shape, low)
        vmem_spec = pl.BlockSpec(memory_space=pltpu.VMEM)
        grads = pl.pallas_call(
            functools.partial(kernel, n, segs, chunk),
            out_shape=(vmem_out,) * 3,
            in_specs=[any_spec] * 4 + [smem_spec] * 3,
            out_specs=(vmem_spec,) * 3,
            scratch_shapes=[
                pltpu.VMEM((4, items, n * rows, width), low),
                pltpu.VMEM((3, items, n * rows, width), low),
                pltpu.VMEM((items, n * rows, n * rows), jnp.float32),
                pltpu.VMEM((items, n * rows, n * rows), low),
                pltpu.VMEM((2, frames) + block, low),
                pltpu.VMEM((2, frames + 2 * WMAX) + block, low),
                pltpu.VMEM((2, 2, WMAX) + block, low),
                pltpu.VMEM((2, 2, WMAX) + block, low),
                pltpu.VMEM((2, frames) + block, jnp.float32),
                dma((4, pieces, n)),
                dma((4, pieces, n)),
                dma((3, pieces, n)),
                dma((3, pieces, n)),
                dma((2, 2)),
                dma((2, 2)),
                dma((2,)),
                dma((2,)),
                dma((7, pieces)),
                dma((4,)),
                pltpu.SemaphoreType.REGULAR((2, n)),
                pltpu.SemaphoreType.REGULAR((2,)),
            ],
            compiler_params=pltpu.CompilerParams(collective_id=0, has_side_effects=True),
        )(*args)
        return pl.pallas_call(
            put_out,
            out_shape=(out, out, out),
            in_specs=[vmem_spec] * 3,
            out_specs=(any_spec,) * 3,
            scratch_shapes=[dma((3,))],
        )(*(pltpu.with_memory_space_constraint(x, pltpu.VMEM) for x in grads))

    heads_spec = P("seg", None, "pos", None)
    return jax.shard_map(
        on_device,
        mesh=mesh,
        in_specs=(heads_spec,) * 4 + (P(),) * 3,
        out_specs=(heads_spec,) * 3,
        check_vma=False,
    )
```
